32 devices in a mesh: groups: 2 (over y), space: 4 (over z), tm: 2 (over x), comp: 2 (over core).
Axes of the slice: x: 2, y: 2, z: 4, core: 2. Of those that a mesh axis runs over, the one named last changes fastest.
Arguments:
- stored: float32 [4096, 4, 3, 512], P(('groups', 'space', 'comp'), 'tm'), parts along dimension 0, may hold values from -6 to 6
- brick_ids: int32 [4096], P(('groups', 'space', 'comp')), parts along dimension 0, may hold values from 0 to 1073741823, as said below
- brick_counts: int32 [16], P(('groups', 'space', 'comp')), parts along dimension 0, may hold values from 0 to 256
- snapshot_ids: int32 [8], P('groups'), parts along dimension 0, may hold values from 999 to 1008, as said below
- between: float32 [2], P('groups'), parts along dimension 0, may hold values from 0.05 to 0.95
- anchor: int32 [6], P('groups'), parts along dimension 0, may hold values from 0 to 1016, as said below
Outputs:
- vorticity: float32 [3, 128, 64, 128], P(None, ('groups', 'space', 'tm'), 'comp'), parts along dimension 1
The draws below stay inside these ranges and needn't reach their ends.
There are 2 independent parts, one for each index of `groups`. The reference program is written for one: setup_inputs(seed, part) draws one part's arguments, and reference() takes and returns one part's arrays. A program takes and returns all parts, laid end to end along the dimension named above; each array names one. Nothing has to cross between parts.
Inputs may be any that keep to these rules, and one draw needn't show every extreme that they name: `brick_ids`: the live slots of each device hold distinct codes, ascending; all live slots together name every brick of the cutout once. Slots past a device's count hold meaningless codes. With a tile being the cells x in [s * 16, (s + 1) * 16) and y in [c * 32, (c + 1) * 32) for device index s * 2 + c over space+comp: one device holds at most 32 bricks of one tile, and the devices of one space index hold exactly 32 bricks of each tile together. `snapshot_ids`: strictly increasing, by 1 to 3 from one to the next; the last is 1008. `anchor`: each entry plus the cutout's extent in bricks along that dimension is at most 1024.
All inputs are finite; a program needn't handle non-finite values.
Results may differ from the reference program's by a relative error of at most 0.00002.
Values sent between devices are 32-bit elements; how exact they have to be, the bound alone decides.
No kernel may reach another device: no remote copies, remote signals or barrier semaphores. Data moves between devices by JAX's collectives and lax.ppermute only.
A program may use at most 128 MiB of HBM per device.

```python
import jax
import jax.numpy as jnp

BRICK = 8
GRID = 1024
SNAPS = 4
NZ = 128
NX = 64
NY = 64
DEVS = 8
TILE_BRICKS = 128
CAP = 32
SLOTS = 256
N_SPACE = 4
N_COMP = 2


def encode_morton(across, along, depth):
    levels = GRID.bit_length() - 1
    morton = jnp.zeros_like(across)
    for level in range(levels):
        morton = morton | (jnp.right_shift(across, level) & 1) << 3 * level + 2
        morton = morton | (jnp.right_shift(along, level) & 1) << 3 * level + 1
        morton = morton | (jnp.right_shift(depth, level) & 1) << 3 * level
    return morton


def brick_layout(key):
    keys = jax.random.split(jax.random.fold_in(key, 7301), 9)
    span_x = NX // BRICK
    span_y = NY // BRICK
    span_z = NZ // BRICK
    spans = (span_x, span_y, span_z)
    narrowest = min(range(3), key=lambda entry: spans[entry])
    starts_drawn = [jax.random.randint(keys[0], (), 0, GRID - span_x + 1), jax.random.randint(keys[7], (), 0, GRID - span_y + 1), jax.random.randint(keys[8], (), 0, GRID - span_z + 1)]
    starts_drawn[narrowest] = jnp.asarray(GRID - spans[narrowest], jnp.int32)
    anchor = jnp.stack(starts_drawn).astype(jnp.int32)
    devices = N_SPACE * N_COMP
    bricks_across = span_x // N_SPACE
    bricks_along = span_y // N_COMP
    bricks_deep = span_z
    scores = jax.random.randint(keys[1], (devices, TILE_BRICKS), 0, 2 ** 30 // TILE_BRICKS) * TILE_BRICKS
    scores = scores + jnp.arange(TILE_BRICKS, dtype=jnp.int32)[None, :]
    order = jnp.argsort(scores, axis=1, stable=True).astype(jnp.int32)
    favored = jax.random.randint(keys[2], (N_SPACE,), 0, 2)
    rolled = jax.random.randint(keys[3], (N_SPACE, devices), 0, 4)
    partial_held = jax.random.randint(keys[4], (N_SPACE, devices), 1, CAP)
    forced = jax.random.randint(keys[5], (), 0, N_SPACE)
    held = jnp.where(rolled < 3, CAP, partial_held)
    held = jnp.where(jnp.arange(N_SPACE)[:, None] == forced, CAP, held)
    ranking = jnp.arange(TILE_BRICKS, dtype=jnp.int32)
    group_of = ranking // CAP
    within = ranking % CAP
    held_rank = held[group_of, :].T
    chosen = favored[group_of][None, :]
    member = jnp.where(within[None, :] < held_rank, chosen, 1 - chosen)
    source = (group_of[None, :] * N_COMP + member).reshape(-1).astype(jnp.int32)
    tile_index = jnp.arange(devices, dtype=jnp.int32)[:, None]
    local_x = tile_index // N_COMP * bricks_across + order // (bricks_along * bricks_deep)
    local_y = tile_index % N_COMP * bricks_along + order // bricks_deep % bricks_along
    local_z = order % bricks_deep
    morton = encode_morton(anchor[0] + local_x, anchor[1] + local_y, anchor[2] + local_z).reshape(-1)
    first = jnp.argsort(morton, stable=True)
    second = jnp.argsort(source[first], stable=True)
    arranged = first[second]
    sorted_source = source[arranged]
    sorted_morton = morton[arranged]
    counts = jax.ops.segment_sum(jnp.ones_like(source), source, num_segments=devices).astype(jnp.int32)
    starts = jnp.cumsum(counts) - counts
    position = jnp.arange(source.shape[0], dtype=jnp.int32) - starts[sorted_source]
    slot_index = sorted_source * SLOTS + position
    filler_keys = jax.random.split(keys[6], 3)
    filler = encode_morton(anchor[0] + jax.random.randint(filler_keys[0], (devices * SLOTS,), 0, span_x), anchor[1] + jax.random.randint(filler_keys[1], (devices * SLOTS,), 0, span_y), anchor[2] + jax.random.randint(filler_keys[2], (devices * SLOTS,), 0, span_z))
    filler = filler.at[SLOTS - 1].set(GRID ** 3 - 1).at[SLOTS - 2].set(0)
    identities = filler.at[slot_index].set(sorted_morton).astype(jnp.int32)
    return (identities, counts, anchor)


def draw_brick_ids(key, part):
    return brick_layout(key)[0]


def draw_brick_counts(key, part):
    return brick_layout(key)[1]


def draw_anchor(key, part):
    return brick_layout(key)[2]


def draw_snapshot_ids(key, part):
    keys = jax.random.split(jax.random.fold_in(key, 911), 2)
    spacings = jax.random.randint(keys[1], (SNAPS,), 1, 4)
    rising = jnp.cumsum(spacings) - spacings[0]
    return (1008 - rising[SNAPS - 1] + rising).astype(jnp.int32)


def block_scale(key, dims, cuts, smallest, largest):
    gain = 1.0
    for dim, shards_of in cuts:
        heights = jax.random.uniform(jax.random.fold_in(jax.random.fold_in(key, 6), dim), (shards_of,), jnp.float32, smallest / len(cuts), largest / len(cuts))
        gain = gain * jnp.repeat(jnp.exp(heights), dims[dim] // shards_of).reshape((-1,) + (1,) * (len(dims) - 1 - dim))
    return gain


def scatter_about(rng, dims, width, bound, cuts=(), kind=jnp.bfloat16):
    entries = jax.random.normal(rng, dims, jnp.float32) * width
    if len(cuts) > 0:
        entries = block_scale(rng, dims, cuts, -0.22, 0.18) * entries
    return jnp.clip(entries, min=-bound, max=bound).astype(kind)


def setup_inputs(seed: int = 0, part: int = 0) -> dict:
    key_of = jax.random.split(jax.random.key(seed), 7)
    own_keys = jax.random.split(jax.random.fold_in(key_of[6], part), 7)
    stored = scatter_about(own_keys[0], (DEVS * SLOTS, SNAPS, 3, BRICK ** 3), 1.0, 6.0, ((0, 8), (1, 2)), jnp.float32)
    brick_ids = draw_brick_ids(jax.random.fold_in(jax.random.fold_in(key_of[6], part), 71), part)
    brick_counts = draw_brick_counts(jax.random.fold_in(jax.random.fold_in(key_of[6], part), 71), part)
    snapshot_ids = draw_snapshot_ids(jax.random.fold_in(jax.random.fold_in(key_of[6], part), 71), part)
    between = jnp.clip(jax.random.uniform(own_keys[4], (1,), jnp.float32, 0.05, 0.95), 0.05, 0.95)
    anchor = draw_anchor(jax.random.fold_in(jax.random.fold_in(key_of[6], part), 71), part)
    return {"stored": stored, "brick_ids": brick_ids, "brick_counts": brick_counts, "snapshot_ids": snapshot_ids, "between": between, "anchor": anchor}


coefficients = (0.8, -0.2, 4.0 / 105.0, -1.0 / 280.0)


def hermite_weights(snapshot_ids, between):
    stamps = snapshot_ids.astype(jnp.float32)
    fraction = between[0]
    square = fraction * fraction
    cubed = square * fraction
    spacing = stamps[2] - stamps[1]
    first_base = 2.0 * cubed - 3.0 * square + 1.0
    first_slope = cubed - 2.0 * square + fraction
    second_base = 3.0 * square - 2.0 * cubed
    second_slope = cubed - square
    left_gain = first_slope * spacing / (stamps[2] - stamps[0])
    right_gain = second_slope * spacing / (stamps[3] - stamps[1])
    return jnp.stack([-left_gain, first_base - right_gain, second_base + left_gain, right_gain])


def decode_morton(morton):
    levels = GRID.bit_length() - 1
    decoded = []
    for offset in (2, 1, 0):
        coordinate = jnp.zeros_like(morton)
        for level in range(levels):
            coordinate = coordinate | ((jnp.right_shift(morton, 3 * level + offset) & 1) << level)
        decoded.append(coordinate)
    return decoded


def periodic(field, axis_number):
    total = 0.0
    for distance, coefficient in enumerate(coefficients, start=1):
        total = total + coefficient * (jnp.roll(field, -distance, axis_number) - jnp.roll(field, distance, axis_number))
    return total


def reference(stored, brick_ids, brick_counts, snapshot_ids, between, anchor):
    weights = hermite_weights(snapshot_ids, between)
    blended = weights[0] * stored[:, 0]
    for snapshot in range(1, SNAPS):
        blended = blended + weights[snapshot] * stored[:, snapshot]
    span_x = NX // BRICK
    span_y = NY // BRICK
    span_z = NZ // BRICK
    across, along, depth = decode_morton(brick_ids)
    local_x = jnp.mod(across - anchor[0], span_x)
    local_y = jnp.mod(along - anchor[1], span_y)
    local_z = jnp.mod(depth - anchor[2], span_z)
    index = ((local_x * span_y + local_y) * span_z + local_z).astype(jnp.int32)
    positions = jnp.arange(brick_ids.shape[0], dtype=jnp.int32)
    owners = positions // SLOTS
    live_flags = (positions % SLOTS) < brick_counts[owners]
    total_bricks = span_x * span_y * span_z
    landing = jnp.where(live_flags, index, total_bricks).astype(jnp.int32)
    grid = jnp.zeros((total_bricks + 1, 3, BRICK ** 3), jnp.float32).at[landing].set(blended)[:total_bricks]
    velocity = grid.reshape(span_x, span_y, span_z, 3, BRICK, BRICK, BRICK)
    velocity = velocity.transpose(3, 0, 4, 1, 5, 2, 6).reshape(3, NX, NY, NZ)
    d_dx = periodic(velocity[1:3], 1)
    d_dy = periodic(velocity[0::2], 2)
    d_dz = periodic(velocity[0:2], 3)
    return jnp.stack([d_dy[1] - d_dz[1], d_dz[0] - d_dx[1], d_dx[0] - d_dy[0]])
```

```python
import functools

import jax
import jax.numpy as jnp
from jax import lax
from jax.experimental import pallas as pl
from jax.experimental.pallas import tpu as pltpu
from jax.sharding import PartitionSpec as P

BRICK = 8
GRID = 1024
CXD = 8
CY = 32
NZ = 128
LANES = 128
ROWS = BRICK**3 // LANES
REACH = 4

coefficients = (0.8, -0.2, 4.0 / 105.0, -1.0 / 280.0)

VMEM = pl.BlockSpec(memory_space=pltpu.VMEM)
SMEM = pl.BlockSpec(memory_space=pltpu.SMEM)
HBM = pl.BlockSpec(memory_space=pl.ANY)
f32 = jnp.float32
bf16 = jnp.bfloat16


def thirds(value):
    high = value.astype(bf16)
    rest = value - high.astype(f32)
    middle = rest.astype(bf16)
    low = (rest - middle.astype(f32)).astype(bf16)
    return high, middle, low


def select_rows(onehot, value):
    total = None
    for part in thirds(value):
        product = jnp.dot(onehot, part, preferred_element_type=f32)
        total = product if total is None else total + product
    return total


def hermite_weights(snapshot_ref, between_ref, first, count):
    shape = (8, LANES)
    stamps = [jnp.full(shape, snapshot_ref[i], jnp.int32).astype(f32) for i in range(4)]
    fraction = jnp.full(shape, between_ref[0], f32)
    square = fraction * fraction
    cubed = square * fraction
    spacing = stamps[2] - stamps[1]
    first_base = 2.0 * cubed - 3.0 * square + 1.0
    first_slope = cubed - 2.0 * square + fraction
    second_base = 3.0 * square - 2.0 * cubed
    second_slope = cubed - square
    left_gain = first_slope * spacing / (stamps[2] - stamps[0])
    right_gain = second_slope * spacing / (stamps[3] - stamps[1])
    weights = [-left_gain, first_base - right_gain, second_base + left_gain, right_gain]
    mine = []
    for offset in range(count):
        value = weights[offset]
        for start in range(count, 4, count):
            value = jnp.where(first == start, weights[start + offset], value)
        mine.append(value[0:1, :])
    return mine


def pack_kernel(sizes, parts, with_meta, *refs):
    (stored_ref, ids_ref, count_ref, snapshot_ref, between_ref, anchor_ref) = refs[:6]
    keep_ref, send_ref = refs[6:8]
    fields = refs[8 : 8 + len(parts)]
    sem = refs[8 + len(parts)]
    space_count, time_count, comp_count, snaps = sizes
    slots = ids_ref.shape[1]
    bricks_across = CXD * time_count // BRICK
    bricks_along = CY // BRICK
    bricks_deep = NZ // BRICK
    tile_bricks = bricks_across * bricks_along * bricks_deep
    capacity = tile_bricks // space_count
    span = ROWS * snaps
    copies = []
    for index, part in enumerate(parts):
        copy = pltpu.make_async_copy(
            stored_ref.at[:, pl.ds(part * span, span), :], fields[index], sem.at[index]
        )
        copy.start()
        copies.append(copy)
    space = lax.axis_index("space")
    comp = lax.axis_index("comp")
    time = lax.axis_index("tm")
    morton = ids_ref[...]
    slot = lax.broadcasted_iota(jnp.int32, (1, slots), 1)
    live = slot < count_ref[0]
    decoded = []
    for offset in (2, 1, 0):
        coordinate = jnp.zeros_like(morton)
        for level in range(GRID.bit_length() - 1):
            bit = lax.shift_right_logical(morton, 2 * level + offset) & (1 << level)
            coordinate = coordinate | bit
        decoded.append(coordinate)
    local_x = (decoded[0] - anchor_ref[0]) & (space_count * bricks_across - 1)
    local_y = (decoded[1] - anchor_ref[1]) & (comp_count * bricks_along - 1)
    local_z = (decoded[2] - anchor_ref[2]) & (bricks_deep - 1)
    hop = (local_x // bricks_across - space) & (space_count - 1)
    side = local_y // bricks_along
    place = local_z * (bricks_across * bricks_along) + (
        local_x % bricks_across
    ) * bricks_along + local_y % bricks_along
    label = jnp.where(live, hop * comp_count + side, -1)
    targets = space_count * comp_count
    tags = lax.broadcasted_iota(jnp.int32, (targets, slots), 0)
    member = jnp.where(tags == label, 1.0, 0.0)
    earlier = jnp.where(
        lax.broadcasted_iota(jnp.int32, (slots, slots), 0)
        < lax.broadcasted_iota(jnp.int32, (slots, slots), 1),
        1.0,
        0.0,
    ).astype(bf16)
    before = jnp.dot(member.astype(bf16), earlier, preferred_element_type=f32)
    rank = jnp.sum(before * member, axis=0, keepdims=True).astype(jnp.int32)
    position = jnp.where(comp == 0, rank, capacity - 1 - rank)
    key = jnp.where(live, hop * capacity + position, -1)
    mine = side == comp
    queue = lax.broadcasted_iota(jnp.int32, (tile_bricks, slots), 0)
    kept = jnp.where((queue == key) & mine, 1.0, 0.0).astype(bf16)
    sent = jnp.where((queue == key) & jnp.logical_not(mine), 1.0, 0.0).astype(bf16)
    onehot = jnp.concatenate([kept, sent], axis=0)
    base = len(parts) * ROWS * capacity
    if with_meta:
        hops = lax.broadcasted_iota(jnp.int32, (max(space_count, 8), slots), 0)
        labelled = jnp.where(hops == hop, place, 0).astype(f32).astype(bf16)
        for matrix, ref in ((kept, keep_ref), (sent, send_ref)):
            meta = lax.dot_general(
                labelled, matrix, (((1,), (1,)), ((), ())), preferred_element_type=f32
            )
            for step in range(space_count):
                ref[step, pl.ds(base, 8), :] = jnp.zeros((8, LANES), f32)
                for piece in range(tile_bricks // LANES):
                    ref[step, pl.ds(base + piece, 1), :] = meta[
                        step : step + 1, piece * LANES : (piece + 1) * LANES
                    ]
    weights = hermite_weights(snapshot_ref, between_ref, time * snaps, snaps)
    for index in range(len(parts)):
        copies[index].wait()
        flat = fields[index].reshape(slots * span, LANES)
        for row in range(ROWS):
            value = None
            for snap in range(snaps):
                term = weights[snap] * flat[pl.ds(row * snaps + snap, slots, stride=span), :]
                value = term if value is None else value + term
            rows = select_rows(onehot, value)
            for half, ref in ((0, keep_ref), (1, send_ref)):
                for step in range(space_count):
                    start = half * tile_bricks + step * capacity
                    ref[step, pl.ds((index * ROWS + row) * capacity, capacity), :] = rows[
                        start : start + capacity, :
                    ]


def swap_blocks(blocks):
    count = len(blocks)
    lane = lax.broadcasted_iota(jnp.int32, blocks[0].shape, 1)
    distance = 1
    while distance < count:
        shift = BRICK * distance
        upper = (lane & shift) != 0
        blocks = list(blocks)
        for index in range(count):
            if index & distance:
                continue
            first, second = blocks[index], blocks[index + distance]
            blocks[index] = jnp.where(upper, pltpu.roll(second, shift, 1), first)
            blocks[index + distance] = jnp.where(
                upper, second, pltpu.roll(first, LANES - shift, 1)
            )
        distance *= 2
    return blocks


def assemble_kernel(sizes, parts, wide, *refs):
    space_count, time_count, comp_count, _ = sizes
    bricks_across = CXD * time_count // BRICK
    bricks_along = CY // BRICK
    bricks_deep = NZ // BRICK
    stack = bricks_across * bricks_along
    tile_bricks = stack * bricks_deep
    capacity = tile_bricks // space_count
    messages = refs[:space_count]
    refs = refs[space_count:]
    if wide:
        places_ref, window_refs, edge_refs = (
            refs[0],
            refs[1 : 1 + time_count],
            refs[1 + time_count : 1 + 2 * time_count],
        )
        base = len(parts) * ROWS * capacity
        places = messages[0][pl.ds(base, 8), :]
        for message in messages[1:]:
            places = places + message[pl.ds(base, 8), :]
        places_ref[...] = places
    else:
        places = refs[0][...]
        window_refs = refs[1 : 1 + time_count]
    slab = refs[-1]
    place = jnp.concatenate(
        [places[piece : piece + 1, :] for piece in range(tile_bricks // LANES)], axis=1
    ).astype(jnp.int32)
    onehot = jnp.where(
        lax.broadcasted_iota(jnp.int32, (tile_bricks, tile_bricks), 0) == place, 1.0, 0.0
    ).astype(bf16)
    for index in range(len(parts)):
        for row in range(ROWS):
            queue = jnp.concatenate(
                [
                    message[pl.ds((index * ROWS + row) * capacity, capacity), :]
                    for message in messages
                ],
                axis=0,
            )
            rows = select_rows(onehot, queue)
            blocks = swap_blocks(
                [rows[deep * stack : (deep + 1) * stack, :] for deep in range(bricks_deep)]
            )
            for cell, block in enumerate(blocks):
                slab[
                    index, row * 2 + cell // BRICK, pl.ds(cell % BRICK, stack, stride=BRICK), :
                ] = block
    time = lax.axis_index("tm")
    own = CXD // BRICK
    for shift in range(time_count):
        target = lax.rem(time + shift, time_count)
        for index in range(len(parts)):
            for x in range(CXD):
                window_refs[shift][index, x] = slab[
                    index, x, pl.ds(pl.multiple_of(target * own * CY, CY), CY), :
                ]
            if wide:
                before, after = target - 1, target + 1
                if time_count == 2:
                    starts = ((jnp.where(target == 0, 0, REACH), 1 - target),)
                else:
                    starts = (
                        (CXD - REACH, jnp.maximum(before, 0)),
                        (0, jnp.minimum(after, time_count - 1)),
                    )
                for piece, (first, block) in enumerate(starts):
                    for x in range(REACH):
                        window_refs[shift][index, CXD + piece * REACH + x] = slab[
                            index, first + x, pl.ds(pl.multiple_of(block * CY, CY), CY), :
                        ]
    if wide:
        for order in range(time_count):
            last = time == order
            first = jnp.where(last, CXD - REACH, 0)
            block = jnp.where(last, bricks_across - 1, 0)
            for index in range(len(parts)):
                for x in range(REACH):
                    edge_refs[order][index, x] = slab[
                        index, first + x, pl.ds(pl.multiple_of(block * CY, CY), CY), :
                    ]


def difference(load):
    total = None
    for distance, coefficient in enumerate(coefficients, start=1):
        term = coefficient * (load(distance) - load(-distance))
        total = term if total is None else total + term
    return total


def along_z(value):
    def shifted(distance):
        return pltpu.roll(value, (-distance) % NZ, value.ndim - 1)

    return difference(shifted)


def curl_kernel(time_count, *refs):
    wide_refs = refs[:time_count]
    narrow_refs = refs[time_count : 2 * time_count]
    edge_refs = refs[2 * time_count : 3 * time_count]
    side_ref, out_ref, across, along = refs[3 * time_count :]

    def summed(group, *index):
        total = group[0][index]
        for ref in group[1:]:
            total = total + ref[index]
        return total

    time = lax.axis_index("tm")
    extra = 1 if time_count == 2 else 2
    for k in range(2):
        for x in range(CXD):
            value = summed(wide_refs, k, x)
            across[k, REACH + x] = value
            if k == 1:
                along[1, x, pl.ds(8, CY), :] = value
        for x in range(REACH):
            halo = summed(edge_refs, k, x)
            inner = summed(wide_refs, k, CXD + x)
            outer = summed(wide_refs, k, CXD + (extra - 1) * REACH + x)
            across[k, x] = jnp.where(time == 0, halo, inner)
            across[k, REACH + CXD + x] = jnp.where(time == time_count - 1, halo, outer)
    for x in range(CXD):
        along[0, x, pl.ds(8, CY), :] = summed(narrow_refs, 0, x)
        for k in range(2):
            along[k, x, pl.ds(0, 8), :] = side_ref[k, x, pl.ds(8, 8), :]
            along[k, x, pl.ds(8 + CY, 8), :] = side_ref[k, x, pl.ds(0, 8), :]
    for x in range(CXD):
        d_dy = [
            difference(lambda m, k=k: along[k, x, pl.ds(8 + m, CY), :]) for k in range(2)
        ]
        d_dx = [difference(lambda m, k=k: across[k, REACH + x + m]) for k in range(2)]
        u_z = along_z(along[0, x, pl.ds(8, CY), :])
        v_z = along_z(across[0, REACH + x])
        out_ref[0, x] = d_dy[1] - v_z
        out_ref[1, x] = u_z - d_dx[1]
        out_ref[2, x] = d_dx[0] - d_dy[0]


def body(stored, brick_ids, brick_counts, snapshot_ids, between, anchor):
    space_count = lax.axis_size("space")
    time_count = lax.axis_size("tm")
    comp_count = lax.axis_size("comp")
    slots, snaps = stored.shape[:2]
    sizes = (space_count, time_count, comp_count, snaps)
    tile_bricks = (CXD * time_count // BRICK) * (CY // BRICK) * (NZ // BRICK)
    capacity = tile_bricks // space_count
    span = ROWS * snaps
    cells = stored.transpose(0, 2, 1, 3).reshape(slots, 3, snaps, ROWS, LANES)
    cells = cells.transpose(0, 1, 3, 2, 4).reshape(slots, 3 * span, LANES)
    ids = brick_ids.reshape(1, slots)
    swap = [(i, comp_count - 1 - i) for i in range(comp_count)]

    def packed(parts, with_meta):
        rows = len(parts) * ROWS * capacity + (8 if with_meta else 0)
        shape = jax.ShapeDtypeStruct((space_count, rows, LANES), f32)
        keep, send = pl.pallas_call(
            functools.partial(pack_kernel, sizes, parts, with_meta),
            out_shape=(shape, shape),
            in_specs=[HBM, VMEM, SMEM, SMEM, SMEM, SMEM],
            out_specs=(VMEM, VMEM),
            scratch_shapes=[pltpu.VMEM((slots, span, LANES), f32) for _ in parts]
            + [pltpu.SemaphoreType.DMA((len(parts),))],
        )(cells, ids, brick_counts, snapshot_ids, between, anchor)
        other = lax.ppermute(send, "comp", swap)
        messages = []
        for hop in range(space_count):
            message = keep[hop] + other[hop]
            if hop > 0:
                ring = [(i, (i + hop) % space_count) for i in range(space_count)]
                message = lax.ppermute(message, "space", ring)
            messages.append(message)
        return messages

    def to_times(windows):
        moved = [windows[0]]
        for shift in range(1, time_count):
            ring = [(i, (i + shift) % time_count) for i in range(time_count)]
            moved.append(lax.ppermute(windows[shift], "tm", ring))
        return moved

    slab_rows = (CXD * time_count // BRICK) * CY
    wide_messages = packed((1, 2), True)
    narrow_messages = packed((0,), False)
    extent = CXD + (REACH if time_count == 2 else 2 * REACH)
    window = jax.ShapeDtypeStruct((2, extent, CY, NZ), f32)
    edge = jax.ShapeDtypeStruct((2, REACH, CY, NZ), f32)
    results = pl.pallas_call(
        functools.partial(assemble_kernel, sizes, (1, 2), True),
        out_shape=[jax.ShapeDtypeStruct((8, LANES), f32)]
        + [window] * time_count
        + [edge] * time_count,
        in_specs=[VMEM] * space_count,
        out_specs=[VMEM] * (1 + 2 * time_count),
        scratch_shapes=[pltpu.VMEM((2, CXD, slab_rows, NZ), f32)],
    )(*wide_messages)
    places = results[0]
    wide = to_times(results[1 : 1 + time_count])
    edges = []
    for order, value in enumerate(results[1 + time_count :]):
        pairs = []
        for s in range(space_count):
            pairs.append((s * time_count + order, (s + 1) % space_count * time_count))
            pairs.append(
                (
                    s * time_count + time_count - 1 - order,
                    (s - 1) % space_count * time_count + time_count - 1,
                )
            )
        edges.append(lax.ppermute(value, ("space", "tm"), pairs))
    small = jax.ShapeDtypeStruct((1, CXD, CY, NZ), f32)
    narrow = pl.pallas_call(
        functools.partial(assemble_kernel, sizes, (0,), False),
        out_shape=[small] * time_count,
        in_specs=[VMEM] * (space_count + 1),
        out_specs=[VMEM] * time_count,
        scratch_shapes=[pltpu.VMEM((1, CXD, slab_rows, NZ), f32)],
    )(*narrow_messages, places)
    narrow = to_times(narrow)

    def sides(group, k):
        low = sum(value[k, :CXD, :8] for value in group)
        high = sum(value[k, :CXD, CY - 8 :] for value in group)
        return jnp.concatenate([low, high], axis=1)

    side = jnp.stack([sides(narrow, 0), sides(wide, 1)])
    side = lax.ppermute(side, "comp", swap)
    return pl.pallas_call(
        functools.partial(curl_kernel, time_count),
        out_shape=jax.ShapeDtypeStruct((3, CXD, CY, NZ), f32),
        in_specs=[VMEM] * (3 * time_count + 1),
        out_specs=VMEM,
        scratch_shapes=[
            pltpu.VMEM((2, CXD + 2 * REACH, CY, NZ), f32),
            pltpu.VMEM((2, CXD, CY + 16, NZ), f32),
        ],
    )(*wide, *narrow, *edges, side)


def solution(mesh):
    return jax.shard_map(
        body,
        mesh=mesh,
        in_specs=(
            P(("groups", "space", "comp"), "tm", None, None),
            P(("groups", "space", "comp")),
            P(("groups", "space", "comp")),
            P("groups"),
            P("groups"),
            P("groups"),
        ),
        out_specs=P(None, ("groups", "space", "tm"), "comp", None),
        check_vma=False,
    )
```

```python
import functools

import jax
import jax.numpy as jnp
from jax import lax
from jax.experimental import pallas as pl
from jax.experimental.pallas import tpu as pltpu
from jax.sharding import PartitionSpec as P


BRICK = 8
GRID = 1024
CXD = 8
CY = 32
NZ = 128
LANES = 128
ROWS = BRICK**3 // LANES
REACH = 4


coefficients = (0.8, -0.2, 4.0 / 105.0, -1.0 / 280.0)

VMEM = pl.BlockSpec(memory_space=pltpu.VMEM)
SMEM = pl.BlockSpec(memory_space=pltpu.SMEM)
HBM = pl.BlockSpec(memory_space=pltpu.HBM)
f32 = jnp.float32
bf16 = jnp.bfloat16
LIMIT = pltpu.CompilerParams(vmem_limit_bytes=16 * 1024 * 1024)


def thirds(value):
    high = value.astype(bf16)
    rest = value - high.astype(f32)
    middle = rest.astype(bf16)
    low = (rest - middle.astype(f32)).astype(bf16)
    return high, middle, low


def select_rows(onehot, value):
    total = None
    for part in thirds(value):
        product = jnp.dot(onehot, part, preferred_element_type=f32)
        total = product if total is None else total + product
    return total


def hermite_weights(snapshot_ref, between_ref, first, count):
    shape = (8, LANES)
    stamps = [jnp.full(shape, snapshot_ref[i], jnp.int32).astype(f32) for i in range(4)]
    fraction = jnp.full(shape, between_ref[0], f32)
    square = fraction * fraction
    cubed = square * fraction
    spacing = stamps[2] - stamps[1]
    first_base = 2.0 * cubed - 3.0 * square + 1.0
    first_slope = cubed - 2.0 * square + fraction
    second_base = 3.0 * square - 2.0 * cubed
    second_slope = cubed - square
    left_gain = first_slope * spacing / (stamps[2] - stamps[0])
    right_gain = second_slope * spacing / (stamps[3] - stamps[1])
    weights = [-left_gain, first_base - right_gain, second_base + left_gain, right_gain]
    mine = []
    for offset in range(count):
        value = weights[offset]
        for start in range(count, 4, count):
            value = jnp.where(first == start, weights[start + offset], value)
        mine.append(value[0:1, :])
    return mine


def pack_rows(sizes, index, load, weights, onehot, refs):
    space_count, _, _, snaps = sizes
    tile_bricks = onehot.shape[0] // len(refs)
    capacity = tile_bricks // space_count
    for row in range(ROWS):
        value = None
        for snap in range(snaps):
            term = weights[snap] * load(row * snaps + snap)
            value = term if value is None else value + term
        rows = select_rows(onehot, value)
        for half, ref in enumerate(refs):
            for step in range(space_count):
                start = half * tile_bricks + step * capacity
                ref[step, pl.ds((index * ROWS + row) * capacity, capacity), :] = rows[
                    start : start + capacity, :
                ]


def pack_kernel(sizes, *refs):
    stored_ref, ids_hbm, snapshot_hbm, anchor_hbm, count_ref, between_ref = refs[:6]
    keep_ref, send_ref, later_ref, onehot_ref, weights_ref = refs[6:11]
    first_ref, second_ref, ids_ref, snapshot_ref, anchor_ref, sem = refs[11:]
    space_count, time_count, comp_count, snaps = sizes
    slots = ids_ref.shape[1]
    bricks_across = CXD * time_count // BRICK
    bricks_along = CY // BRICK
    bricks_deep = NZ // BRICK
    tile_bricks = bricks_across * bricks_along * bricks_deep
    capacity = tile_bricks // space_count
    span = ROWS * snaps
    pairs = [(ids_hbm, ids_ref), (snapshot_hbm, snapshot_ref), (anchor_hbm, anchor_ref)]
    for part, field in ((1, first_ref), (2, second_ref), (0, later_ref)):
        pairs.append((stored_ref.at[:, pl.ds(part * span, span), :], field))
    copies = [
        pltpu.make_async_copy(source, target, sem.at[index])
        for index, (source, target) in enumerate(pairs)
    ]
    for copy in copies:
        copy.start()
    space = lax.axis_index("space")
    comp = lax.axis_index("comp")
    time = lax.axis_index("tm")
    earlier = jnp.where(
        lax.broadcasted_iota(jnp.int32, (slots, slots), 0)
        < lax.broadcasted_iota(jnp.int32, (slots, slots), 1),
        1.0,
        0.0,
    ).astype(bf16)
    for copy in copies[:3]:
        copy.wait()
    weights = hermite_weights(snapshot_ref, between_ref, time * snaps, snaps)
    for snap in range(snaps):
        weights_ref[pl.ds(snap, 1), :] = weights[snap]
    morton = ids_ref[...]
    slot = lax.broadcasted_iota(jnp.int32, (1, slots), 1)
    live = slot < count_ref[0]
    decoded = []
    for offset in (2, 1, 0):
        coordinate = jnp.zeros_like(morton)
        for level in range(GRID.bit_length() - 1):
            bit = lax.shift_right_logical(morton, 2 * level + offset) & (1 << level)
            coordinate = coordinate | bit
        decoded.append(coordinate)
    local_x = (decoded[0] - anchor_ref[0]) & (space_count * bricks_across - 1)
    local_y = (decoded[1] - anchor_ref[1]) & (comp_count * bricks_along - 1)
    local_z = (decoded[2] - anchor_ref[2]) & (bricks_deep - 1)
    hop = (local_x // bricks_across) ^ space
    side = local_y // bricks_along
    place = local_z * (bricks_across * bricks_along) + (
        local_x % bricks_across
    ) * bricks_along + local_y % bricks_along
    label = jnp.where(live, hop * comp_count + side, -1)
    tags = lax.broadcasted_iota(jnp.int32, (space_count * comp_count, slots), 0)
    member = jnp.where(tags == label, 1.0, 0.0)
    before = jnp.dot(member.astype(bf16), earlier, preferred_element_type=f32)
    rank = jnp.sum(before * member, axis=0, keepdims=True).astype(jnp.int32)
    position = jnp.where(comp == 0, rank, capacity - 1 - rank)
    key = jnp.where(live, hop * capacity + position, -1)
    mine = side == comp
    kept_key = jnp.where(mine, key, -1)
    sent_key = jnp.where(mine, -1, key)
    queue = lax.broadcasted_iota(jnp.int32, (tile_bricks, slots), 0)
    kept = jnp.where(queue == kept_key, 1.0, 0.0).astype(bf16)
    sent = jnp.where(queue == sent_key, 1.0, 0.0).astype(bf16)
    onehot = jnp.concatenate([kept, sent], axis=0)
    onehot_ref[...] = onehot
    base = 2 * ROWS * capacity
    hops = lax.broadcasted_iota(jnp.int32, (max(space_count, 8), slots), 0)
    labelled = jnp.where(hops == hop, place, 0).astype(f32).astype(bf16)
    metas = lax.dot_general(
        labelled, onehot, (((1,), (1,)), ((), ())), preferred_element_type=f32
    )
    for half, ref in ((0, keep_ref), (1, send_ref)):
        for step in range(space_count):
            ref[step, pl.ds(base, 8), :] = jnp.zeros((8, LANES), f32)
            for piece in range(tile_bricks // LANES):
                start = half * tile_bricks + piece * LANES
                ref[step, pl.ds(base + piece, 1), :] = metas[
                    step : step + 1, start : start + LANES
                ]
    for index, field in enumerate((first_ref, second_ref)):
        copies[3 + index].wait()
        flat = field.reshape(slots * span, LANES)
        pack_rows(
            sizes,
            index,
            lambda row, flat=flat: flat[pl.ds(row, slots, stride=span), :],
            weights,
            onehot,
            (keep_ref, send_ref),
        )
    copies[5].wait()


def pack_later_kernel(sizes, field_ref, onehot_ref, weights_ref, keep_ref, send_ref):
    snaps = sizes[3]
    slots, span = field_ref.shape[:2]
    flat = field_ref.reshape(slots * span, LANES)
    pack_rows(
        sizes,
        0,
        lambda row: flat[pl.ds(row, slots, stride=span), :],
        [weights_ref[pl.ds(snap, 1), :] for snap in range(snaps)],
        onehot_ref[...],
        (keep_ref, send_ref),
    )


def swap_blocks(blocks):
    count = len(blocks)
    lane = lax.broadcasted_iota(jnp.int32, blocks[0].shape, 1)
    distance = 1
    while distance < count:
        shift = BRICK * distance
        upper = (lane & shift) != 0
        blocks = list(blocks)
        for index in range(count):
            if index & distance:
                continue
            first, second = blocks[index], blocks[index + distance]
            blocks[index] = jnp.where(upper, pltpu.roll(second, shift, 1), first)
            blocks[index + distance] = jnp.where(
                upper, second, pltpu.roll(first, LANES - shift, 1)
            )
        distance *= 2
    return blocks


def assemble_kernel(sizes, parts, wide, *refs):
    space_count, time_count, _, _ = sizes
    bricks_across = CXD * time_count // BRICK
    bricks_along = CY // BRICK
    bricks_deep = NZ // BRICK
    stack = bricks_across * bricks_along
    tile_bricks = stack * bricks_deep
    capacity = tile_bricks // space_count
    messages = refs[:space_count]
    refs = refs[space_count:]
    if wide:
        places_ref, window_refs, edge_refs = (
            refs[0],
            refs[1 : 1 + time_count],
            refs[1 + time_count : 1 + 2 * time_count],
        )
        base = len(parts) * ROWS * capacity
        places = messages[0][pl.ds(base, 8), :]
        for message in messages[1:]:
            places = places + message[pl.ds(base, 8), :]
        places_ref[...] = places
    else:
        places = refs[0][...]
        window_refs = refs[1:2]
    slab = refs[-1]
    place = jnp.concatenate(
        [places[piece : piece + 1, :] for piece in range(tile_bricks // LANES)], axis=1
    ).astype(jnp.int32)
    onehot = jnp.where(
        lax.broadcasted_iota(jnp.int32, (tile_bricks, tile_bricks), 0) == place, 1.0, 0.0
    ).astype(bf16)
    for index in range(len(parts)):
        for row in range(ROWS):
            queue = jnp.concatenate(
                [
                    message[pl.ds((index * ROWS + row) * capacity, capacity), :]
                    for message in messages
                ],
                axis=0,
            )
            rows = select_rows(onehot, queue)
            blocks = swap_blocks(
                [rows[deep * stack : (deep + 1) * stack, :] for deep in range(bricks_deep)]
            )
            for cell, block in enumerate(blocks):
                slab[
                    index, row * 2 + cell // BRICK, pl.ds(cell % BRICK, stack, stride=BRICK), :
                ] = block
    time = lax.axis_index("tm")
    own = CXD // BRICK
    for shift in range(len(window_refs)):
        target = lax.rem(time + shift, time_count)
        for index in range(len(parts)):
            for x in range(CXD):
                window_refs[shift][index, x] = slab[
                    index, x, pl.ds(pl.multiple_of(target * own * CY, CY), CY), :
                ]
            if wide:
                before, after = target - 1, target + 1
                if time_count == 2:
                    starts = ((jnp.where(target == 0, 0, REACH), 1 - target),)
                else:
                    starts = (
                        (CXD - REACH, jnp.maximum(before, 0)),
                        (0, jnp.minimum(after, time_count - 1)),
                    )
                for piece, (first, block) in enumerate(starts):
                    for x in range(REACH):
                        window_refs[shift][index, CXD + piece * REACH + x] = slab[
                            index, first + x, pl.ds(pl.multiple_of(block * CY, CY), CY), :
                        ]
    if wide:
        for shift in range(time_count):
            last = lax.rem(time + shift, time_count) == 0
            first = jnp.where(last, CXD - REACH, 0)
            block = jnp.where(last, bricks_across - 1, 0)
            for index in range(len(parts)):
                for x in range(REACH):
                    edge_refs[shift][index, x] = slab[
                        index, first + x, pl.ds(pl.multiple_of(block * CY, CY), CY), :
                    ]


def own_kernel(*refs):
    refs[-1][...] = sum(ref[0] for ref in refs[:-1])


def difference(load):
    total = None
    for distance, coefficient in enumerate(coefficients, start=1):
        term = coefficient * (load(distance) - load(-distance))
        total = term if total is None else total + term
    return total


def along_z(value):
    def shifted(distance):
        return pltpu.roll(value, (-distance) % NZ, value.ndim - 1)

    return difference(shifted)


def curl_kernel(time_count, *refs):
    wide_refs = refs[:time_count]
    narrow_ref = refs[time_count]
    edge_ref, narrow_side_ref, wide_side_ref, out_ref, across, along = refs[time_count + 1 :]

    def summed(group, *index):
        total = group[0][index]
        for ref in group[1:]:
            total = total + ref[index]
        return total

    time = lax.axis_index("tm")
    extra = 1 if time_count == 2 else 2
    for k in range(2):
        for x in range(CXD):
            value = summed(wide_refs, k, x)
            across[k, REACH + x] = value
            if k == 1:
                along[1, x, pl.ds(8, CY), :] = value
        for x in range(REACH):
            halo = edge_ref[k, x]
            inner = summed(wide_refs, k, CXD + x)
            outer = summed(wide_refs, k, CXD + (extra - 1) * REACH + x)
            across[k, x] = jnp.where(time == 0, halo, inner)
            across[k, REACH + CXD + x] = jnp.where(time == time_count - 1, halo, outer)
    for x in range(CXD):
        along[0, x, pl.ds(8, CY), :] = narrow_ref[0, x]
        for k, ref in enumerate((narrow_side_ref, wide_side_ref)):
            along[k, x, pl.ds(0, 8), :] = ref[x, pl.ds(8, 8), :]
            along[k, x, pl.ds(8 + CY, 8), :] = ref[x, pl.ds(0, 8), :]
    for x in range(CXD):
        d_dy = [
            difference(lambda m, k=k: along[k, x, pl.ds(8 + m, CY), :]) for k in range(2)
        ]
        d_dx = [difference(lambda m, k=k: across[k, REACH + x + m]) for k in range(2)]
        u_z = along_z(along[0, x, pl.ds(8, CY), :])
        v_z = along_z(across[0, REACH + x])
        out_ref[0, x] = d_dy[1] - v_z
        out_ref[1, x] = u_z - d_dx[1]
        out_ref[2, x] = d_dx[0] - d_dy[0]


def body(stored, brick_ids, brick_counts, snapshot_ids, between, anchor):
    space_count = lax.axis_size("space")
    time_count = lax.axis_size("tm")
    comp_count = lax.axis_size("comp")
    slots, snaps = stored.shape[:2]
    sizes = (space_count, time_count, comp_count, snaps)
    bricks_across = CXD * time_count // BRICK
    tile_bricks = bricks_across * (CY // BRICK) * (NZ // BRICK)
    capacity = tile_bricks // space_count
    span = ROWS * snaps
    cells = stored.transpose(0, 2, 1, 3).reshape(slots, 3, snaps, ROWS, LANES)
    cells = cells.transpose(0, 1, 3, 2, 4).reshape(slots, 3 * span, LANES)
    ids = brick_ids.reshape(1, slots)
    held = [
        pltpu.with_memory_space_constraint(value, pltpu.HBM)
        for value in (cells, ids, snapshot_ids, anchor)
    ]
    swap = [(i, comp_count - 1 - i) for i in range(comp_count)]

    def to_places(messages):
        moved = [messages[0]]
        for hop in range(1, space_count):
            ring = [(i, i ^ hop) for i in range(space_count)]
            moved.append(lax.ppermute(messages[hop], "space", ring))
        return moved

    def to_times(windows):
        moved = [windows[0]]
        for shift in range(1, time_count):
            ring = [(i, (i + shift) % time_count) for i in range(time_count)]
            value = windows[shift % len(windows)]
            moved.append(lax.ppermute(value, "tm", ring))
        return moved

    wide_rows = 2 * ROWS * capacity + 8
    field = (slots, span, LANES)
    wide_shape = jax.ShapeDtypeStruct((space_count, wide_rows, LANES), f32)
    keep, send, later, onehot, weights = pl.pallas_call(
        functools.partial(pack_kernel, sizes),
        out_shape=(
            wide_shape,
            wide_shape,
            jax.ShapeDtypeStruct(field, f32),
            jax.ShapeDtypeStruct((2 * tile_bricks, slots), bf16),
            jax.ShapeDtypeStruct((8, LANES), f32),
        ),
        in_specs=[HBM] * 4 + [SMEM] * 2,
        out_specs=(VMEM,) * 5,
        scratch_shapes=[
            pltpu.VMEM(field, f32),
            pltpu.VMEM(field, f32),
            pltpu.VMEM(ids.shape, jnp.int32),
            pltpu.SMEM(snapshot_ids.shape, jnp.int32),
            pltpu.SMEM(anchor.shape, jnp.int32),
            pltpu.SemaphoreType.DMA((6,)),
        ],
        compiler_params=LIMIT,
    )(*held, brick_counts, between)
    other = lax.ppermute(send, "comp", swap)
    wide_messages = to_places([keep[hop] + other[hop] for hop in range(space_count)])

    narrow_shape = jax.ShapeDtypeStruct((space_count, ROWS * capacity, LANES), f32)
    keep, send = pl.pallas_call(
        functools.partial(pack_later_kernel, sizes),
        out_shape=(narrow_shape,) * 2,
        in_specs=[VMEM] * 3,
        out_specs=(VMEM,) * 2,
        compiler_params=LIMIT,
    )(later, onehot, weights)
    partial = keep + lax.ppermute(send, "comp", swap)
    shares = to_times([partial])
    whole = [sum(share[hop] for share in shares) for hop in range(1, space_count)]

    slab_rows = bricks_across * CY
    extent = CXD + (REACH if time_count == 2 else 2 * REACH)
    window = jax.ShapeDtypeStruct((2, extent, CY, NZ), f32)
    edge = jax.ShapeDtypeStruct((2, REACH, CY, NZ), f32)
    results = pl.pallas_call(
        functools.partial(assemble_kernel, sizes, (1, 2), True),
        out_shape=[jax.ShapeDtypeStruct((8, LANES), f32)]
        + [window] * time_count
        + [edge] * time_count,
        in_specs=[VMEM] * space_count,
        out_specs=[VMEM] * (1 + 2 * time_count),
        scratch_shapes=[pltpu.VMEM((2, CXD, slab_rows, NZ), f32)],
        compiler_params=LIMIT,
    )(*wide_messages)
    whole, results = lax.optimization_barrier((whole, results))
    places = results[0]
    edge = to_times(results[1 + time_count :])
    edge = sum(edge[1:], edge[0])
    wide = to_times(results[1 : 1 + time_count])
    pairs = []
    for s in range(space_count):
        pairs.append((s * time_count, (s + 1) % space_count * time_count))
        last = time_count - 1
        pairs.append((s * time_count + last, (s - 1) % space_count * time_count + last))
    edge = lax.ppermute(edge, ("space", "tm"), pairs)
    own = pl.pallas_call(
        own_kernel,
        out_shape=jax.ShapeDtypeStruct(partial.shape[1:], f32),
        in_specs=[VMEM] * time_count,
        out_specs=VMEM,
        compiler_params=LIMIT,
    )(*shares)
    narrow_messages = to_places([own, *whole])
    narrow = pl.pallas_call(
        functools.partial(assemble_kernel, sizes, (0,), False),
        out_shape=[jax.ShapeDtypeStruct((1, CXD, CY, NZ), f32)],
        in_specs=[VMEM] * (space_count + 1),
        out_specs=[VMEM],
        scratch_shapes=[pltpu.VMEM((1, CXD, slab_rows, NZ), f32)],
        compiler_params=LIMIT,
    )(*narrow_messages, places)

    def sides(group, k):
        low = sum(value[k, :CXD, :8] for value in group)
        high = sum(value[k, :CXD, CY - 8 :] for value in group)
        return lax.ppermute(jnp.concatenate([low, high], axis=1), "comp", swap)

    return pl.pallas_call(
        functools.partial(curl_kernel, time_count),
        out_shape=jax.ShapeDtypeStruct((3, CXD, CY, NZ), f32),
        in_specs=[VMEM] * (time_count + 4),
        out_specs=VMEM,
        scratch_shapes=[
            pltpu.VMEM((2, CXD + 2 * REACH, CY, NZ), f32),
            pltpu.VMEM((2, CXD, CY + 16, NZ), f32),
        ],
        compiler_params=LIMIT,
    )(*wide, *narrow, edge, sides(narrow, 0), sides(wide, 1))


def solution(mesh):
    return jax.shard_map(
        body,
        mesh=mesh,
        in_specs=(
            P(("groups", "space", "comp"), "tm", None, None),
            P(("groups", "space", "comp")),
            P(("groups", "space", "comp")),
            P("groups"),
            P("groups"),
            P("groups"),
        ),
        out_specs=P(None, ("groups", "space", "tm"), "comp", None),
        check_vma=False,
    )
```
